1024 devices in a mesh: blk: 8 (over x), wide: 128 (over y, z, core).
Axes of the slice: x: 8, y: 8, z: 8, core: 2. Of those that a mesh axis runs over, the one named last changes fastest.
Arguments:
- upstream: bfloat16 [49152, 7168], P('wide'), may hold values from -8 to 8
- gate_pre: bfloat16 [49152, 1024], P('wide', 'blk'), may hold values from -6 to 6
- up_pre: bfloat16 [49152, 1024], P('wide', 'blk'), may hold values from -8 to 8
- down_weight: bfloat16 [7168, 2, 1024], P(None, None, 'blk'), may hold values from -0.1875 to 0.1875
- block_expert: int32 [384], P('wide'), may hold values from 0 to 1
- row_token: int32 [49152], P('wide'), may hold values from 0 to 383, as said below
- gate_prob: float32 [49152], P('wide'), may hold values from 0.05 to 0.8
Outputs:
- down_grad: float32 [7168, 2, 1024], P('wide', None, 'blk')
- grad_rms: float32 [2], replicated
- prob_grad: float32 [49152], P('wide')
- gate_grad: bfloat16 [49152, 1024], P('wide', 'blk')
- up_grad: bfloat16 [49152, 1024], P('wide', 'blk')
The draws below stay inside these ranges and needn't reach their ends.
Inputs may be any that keep to these rules, and one draw needn't show every extreme that they name: Within each index of wide, row_token is a permutation of the 384 tokens held there: every token has exactly one routed row in the window.
All inputs are finite; a program needn't handle non-finite values.
Results may differ from the reference program's by a relative error of at most 0.0029.
Values sent between devices are 32-bit elements; how exact they have to be, the bound alone decides.
A program may use at most 64 MiB of HBM per device.

```python
import math
import jax
import jax.numpy as jnp
from jax import lax

D = 7168
FFW = 1024
EXPERTS = 2
BLOCK = 128
ROWS = 384
ROWS_ALL = 49152
BLOCKS_ALL = 384


def draw_upstream(key, part):
    first_key, second_key = jax.random.split(key, 2)
    position = jnp.arange(D, dtype=jnp.float32) / (D - 1)
    trend = 1.0 + 2.0 * position
    base = jax.random.normal(first_key, (ROWS_ALL, D), jnp.float32)
    spread = jnp.exp(jax.random.uniform(second_key, (1, D), jnp.float32, 0.0, math.log(10.0)))
    return jnp.clip(0.04 * base * trend[None, :] * spread, -8.0, 8.0).astype(jnp.bfloat16)


def draw_up_pre(key, part):
    first_key, second_key = jax.random.split(key, 2)
    position = jnp.arange(FFW, dtype=jnp.float32) / (FFW - 1)
    trend = 1.0 + 2.0 * position
    base = jax.random.normal(first_key, (ROWS_ALL, FFW), jnp.float32)
    spread = jnp.exp(jax.random.uniform(second_key, (1, FFW), jnp.float32, math.log(0.3), math.log(3.0)))
    return jnp.clip(0.5 * base * trend[None, :] * spread, -8.0, 8.0).astype(jnp.bfloat16)


def draw_row_token(key, part):
    device_keys = jax.random.split(key, ROWS_ALL // ROWS)

    def one_device(device_key):
        return jax.random.permutation(device_key, ROWS)
    return jax.vmap(one_device)(device_keys).reshape(ROWS_ALL).astype(jnp.int32)


def plant(result, rng, low, high):
    spot = [jax.random.randint(jax.random.fold_in(rng, axis), (), 0, length) for axis, length in enumerate(result.shape)]
    widest = result.shape.index(max(result.shape))
    next_to = spot[:widest] + [(spot[widest] + 1) % result.shape[widest]] + spot[widest + 1:]
    return result.at[tuple(spot)].set(low).at[tuple(next_to)].set(high)


def block_scale(own_key, extent, cuts, least, top_value):
    def one(dim, shards_of):
        steps = jax.random.uniform(jax.random.fold_in(jax.random.fold_in(own_key, 6), dim), (shards_of,), jnp.float32, least / len(cuts), top_value / len(cuts))
        return jnp.repeat(jnp.exp(steps), extent[dim] // shards_of).reshape((-1,) + (1,) * (len(extent) - dim - 1))

    level = one(*cuts[0])
    for cut in cuts[1:]:
        level = level * one(*cut)
    return level


def bell_draw(key, extent, scale, bound, cuts=(), kind=jnp.bfloat16):
    drawn = jax.random.normal(key, extent, jnp.float32) * scale
    if len(cuts) > 0:
        drawn = block_scale(key, extent, cuts, -0.22, 0.18) * drawn
    return jnp.clip(drawn, min=-bound, max=bound).astype(kind)


def setup_inputs(seed: int = 0) -> dict:
    key_of = jax.random.split(jax.random.key(seed), 8)
    upstream = draw_upstream(jax.random.fold_in(key_of[7], 71), 0)
    gate_pre = bell_draw(key_of[1], (ROWS_ALL, FFW), 1.0, 6.0, ((0, 128), (1, 8)))
    up_pre = draw_up_pre(jax.random.fold_in(key_of[7], 71), 0)
    down_weight = bell_draw(key_of[3], (D, EXPERTS, FFW), FFW ** -0.5, 0.1875, ((2, 8),))
    block_expert = plant(jax.random.randint(key_of[4], (BLOCKS_ALL,), 0, EXPERTS), jax.random.fold_in(key_of[4], 1), 0, EXPERTS - 1).astype(jnp.int32)
    row_token = draw_row_token(jax.random.fold_in(key_of[7], 71), 0)
    gate_prob = jnp.clip(0.05 + 0.75 * jax.random.uniform(key_of[6], (ROWS_ALL,), jnp.float32) ** block_scale(key_of[6], (ROWS_ALL,), ((0, 128),), -0.2, 0.2), 0.05, 0.8)
    return dict(upstream=upstream, gate_pre=gate_pre, up_pre=up_pre, down_weight=down_weight, block_expert=block_expert, row_token=row_token, gate_prob=gate_prob)


def reference(upstream, gate_pre, up_pre, down_weight, block_expert, row_token, gate_prob):
    owner = jnp.arange(ROWS_ALL, dtype=jnp.int32) // ROWS
    token_index = (owner * ROWS + row_token.astype(jnp.int32)).astype(jnp.int32)
    routed = upstream[token_index]
    gate_value = gate_pre.astype(jnp.float32)
    up_value = up_pre.astype(jnp.float32)
    sigmoid_gate = jax.nn.sigmoid(gate_value)
    active = gate_value * sigmoid_gate
    hidden = active * up_value
    weighted = (hidden * gate_prob[:, None]).astype(jnp.bfloat16)
    routed_blocks = routed.reshape(BLOCKS_ALL, BLOCK, D)
    weighted_blocks = weighted.reshape(BLOCKS_ALL, BLOCK, FFW)

    def project(block_item):
        rows_block, expert_id = block_item
        weights = lax.dynamic_index_in_dim(down_weight, expert_id, 1, keepdims=False)
        return jnp.dot(rows_block, weights, preferred_element_type=jnp.float32)
    projected = lax.map(project, (routed_blocks, block_expert)).reshape(ROWS_ALL, FFW)
    scaled = gate_prob[:, None] * projected
    up_grad = (scaled * active).astype(jnp.bfloat16)
    gate_grad = (scaled * up_value * sigmoid_gate * (1.0 + gate_value * (1.0 - sigmoid_gate))).astype(jnp.bfloat16)
    prob_grad = lax.optimization_barrier(jnp.sum(hidden * projected, axis=1))

    def accumulate(running, block_item):
        rows_block, weighted_block, expert_id = block_item
        product = jnp.dot(rows_block.T, weighted_block, preferred_element_type=jnp.float32)
        current = lax.dynamic_index_in_dim(running, expert_id, 1, keepdims=True)
        return (lax.dynamic_update_index_in_dim(running, current + product[:, None, :], expert_id, 1), None)
    down_grad, _ = lax.scan(accumulate, jnp.zeros((D, EXPERTS, FFW), jnp.float32), (routed_blocks, weighted_blocks, block_expert))
    grad_rms = jnp.sqrt(lax.optimization_barrier(jnp.mean(down_grad * down_grad, axis=(0, 2))))
    return (down_grad, grad_rms, prob_grad, gate_grad, up_grad)
```

```python
import functools

import jax
import jax.numpy as jnp
from jax import lax
from jax.experimental import pallas as pl
from jax.experimental.pallas import tpu as pltpu
from jax.sharding import PartitionSpec as P

D = 7168
FFW = 1024
BLOCK = 128
ROWS = 384
NBLK = 3
F = 128
SIDE = 8
PIECE = 56
COLS = 896
F32 = jnp.float32
BF16 = jnp.bfloat16
MESH = pl.DeviceIdType.MESH


def ring_offset(j):
    far = 4 - (j + 1) // 2
    odd = j % 2
    return (odd * far + (1 - odd) * (8 - far)) % 8


def across(row):
    return jnp.transpose(jnp.broadcast_to(row, (F, F)))


def kernel(
    u_hbm, w_hbm, gate_ref, up_ref, prob_ref, tok_ref, expert_ref,
    down_ref, rms_ref, pgrad_ref, ggrad_ref, ugrad_ref,
    ub, wv, g, r0, rc1, rc2, wf, pacc, wp, oh, pslot, qxc, qy, qz,
    usem, wsem, pair_send, r0_sem, ring_send, rc1_sem, rc2_sem,
    p_send, p_recv, xc_send, xc_recv, y_send, y_recv, z_send, z_recv,
):
    x = lax.axis_index("blk")
    wide = lax.axis_index("wide")
    c = wide % 2
    chip = wide // 2
    y = chip // SIDE
    z = chip % SIDE
    p = (1 - c) * y + c * z
    q = (1 - c) * z + c * y
    a = 8 - 7 * c
    b = 1 + 7 * c

    def block_copy(i):
        yi = (y + ring_offset(i)) % SIDE
        cols = pl.ds(pl.multiple_of(yi * COLS, 128), COLS)
        return pltpu.make_async_copy(u_hbm.at[:, cols], ub.at[i], usem.at[i])

    @pl.loop(0, SIDE)
    def _(i):
        block_copy(i).start()

    w_copy = pltpu.make_async_copy(w_hbm, wv, wsem)
    w_copy.start()

    barrier = pltpu.get_barrier_semaphore()

    def greet(xi, wi):
        pl.semaphore_signal(barrier, inc=1, device_id=(xi, wi), device_id_type=MESH)

    @pl.loop(1, SIDE)
    def _(o):
        greet((x + o) % SIDE, wide)
        greet((x + o) % SIDE, chip * 2 + 1 - c)
        greet(x, (((y + o) % SIDE) * SIDE + z) * 2 + c)
        greet(x, (y * SIDE + (z + o) % SIDE) * 2 + c)

    greet(x, chip * 2 + 1 - c)

    total = jnp.zeros((ROWS, 2 * F), F32)
    token_iota = lax.broadcasted_iota(jnp.int32, (ROWS, F), 0)
    for k in range(NBLK):
        rows = pl.ds(k * BLOCK, BLOCK)
        gate = gate_ref[rows, :].astype(F32)
        up = up_ref[rows, :].astype(F32)
        hidden = gate * jax.nn.sigmoid(gate) * up
        weighted = (hidden * across(prob_ref[pl.ds(k, 1), :])).astype(BF16).astype(F32)
        expert = jnp.full((F, F), expert_ref[k], jnp.int32)
        both = jnp.concatenate(
            [jnp.where(expert == e, weighted, 0.0) for e in range(2)], axis=1
        ).astype(BF16)
        hot = jnp.where(token_iota == tok_ref[pl.ds(k, 1), :], 1.0, 0.0).astype(BF16)
        oh[k] = hot
        total = total + jnp.dot(hot, both, preferred_element_type=F32)
    wp[...] = total.astype(BF16)

    pl.semaphore_wait(barrier, 4 * (SIDE - 1) + 1)

    def pair_copy(idx):
        return pltpu.make_async_remote_copy(
            src_ref=g.at[idx, 1 - c],
            dst_ref=r0.at[idx],
            send_sem=pair_send,
            recv_sem=r0_sem.at[idx],
            device_id=(x, chip * 2 + 1 - c),
            device_id_type=MESH,
        )

    @pl.loop(0, SIDE)
    def _(i):
        block_copy(i).wait()
        yi = (y + ring_offset(i)) % SIDE
        value = lax.dot_general(
            ub[i], wp[...], (((0,), (0,)), ((), ())), preferred_element_type=F32
        )
        g[pl.ds(yi * SIDE, SIDE)] = value.reshape(SIDE, 2, PIECE, 2 * F)

        @pl.loop(0, SIDE)
        def _(zi):
            pair_copy(yi * SIDE + zi).start()

    w_copy.wait()
    pacc[...] = jnp.zeros_like(pacc)

    def slot(d, k, j):
        return (d * 4 + k - 1) * SIDE + j

    def first_copy(d, k, j, idx):
        step = 1 if d == 0 else SIDE - 1
        to = (a * ((p + step) % SIDE) + b * q) * 2 + c
        s = slot(d, k, j)
        return pltpu.make_async_remote_copy(
            src_ref=r0.at[idx],
            dst_ref=rc1.at[s],
            send_sem=ring_send,
            recv_sem=rc1_sem.at[s],
            device_id=(x, to),
            device_id_type=MESH,
        )

    def first_send(d, k, j, more):
        step = 1 if d == 0 else SIDE - 1
        idx = a * ((p + step * k) % SIDE) + b * ((q + ring_offset(j)) % SIDE)
        pair_copy(idx).wait_recv()
        value = r0[idx] + g[idx, c]
        if more:
            first_copy(d, k + 1, j, idx).wait_recv()
            value = value + rc1[slot(d, k + 1, j)]
        r0[idx] = value
        first_copy(d, k, j, idx).start()

    def project(i):
        yi = (y + ring_offset(i)) % SIDE
        wf[...] = wv[pl.ds(pl.multiple_of(yi * 2 * COLS, 16), 2 * COLS), :].astype(F32)
        weight = jnp.concatenate(
            [wf[pl.ds(e, COLS, stride=2), :].astype(BF16) for e in range(2)], axis=1
        )
        pacc[...] += jnp.dot(ub[i], weight, preferred_element_type=F32)

    @pl.loop(0, 4)
    def _(j):
        first_send(0, 4, j + 4, False)
        first_send(1, 4, j, False)

    @pl.loop(0, 4)
    def _(j):
        first_send(0, 3, j, False)
        first_send(1, 3, j + 4, False)

    @pl.loop(0, 4)
    def _(j):
        first_send(0, 3, j + 4, True)
        first_send(1, 3, j, True)

    @pl.loop(0, 4)
    def _(j):
        for h in range(2):
            first_send(0, 2, 2 * j + h, True)
            first_send(1, 2, (2 * j + h + 4) % SIDE, True)
        project(j)

    @pl.loop(0, 4)
    def _(j):
        for h in range(2):
            first_send(0, 1, 2 * j + h, True)
            first_send(1, 1, 2 * j + h, True)
        project(j + 4)

    high = pacc[...].astype(BF16)
    rest = pacc[...] - high.astype(F32)
    middle = rest.astype(BF16)
    low = (rest - middle.astype(F32)).astype(BF16)
    pslot[x] = jnp.zeros((8, F), F32)
    for k in range(NBLK):
        rows = pl.ds(k * BLOCK, BLOCK)
        hot = oh[k]
        moved = sum(
            lax.dot_general(hot, term, (((0,), (0,)), ((), ())), preferred_element_type=F32)
            for term in (low, middle, high)
        )
        expert = jnp.full((F, F), expert_ref[k], jnp.int32)
        projected = jnp.where(expert == 0, moved[:, :F], moved[:, F:])
        gate = gate_ref[rows, :].astype(F32)
        up = up_ref[rows, :].astype(F32)
        sig = jax.nn.sigmoid(gate)
        active = gate * sig
        scaled = across(prob_ref[pl.ds(k, 1), :]) * projected
        ugrad_ref[rows, :] = (scaled * active).astype(BF16)
        ggrad_ref[rows, :] = (scaled * up * sig * (1.0 + gate * (1.0 - sig))).astype(BF16)
        part = jnp.transpose(active * up * projected)
        pslot[x, pl.ds(k, 1), :] = jnp.sum(part, axis=0, keepdims=True)

    def p_copy(s, to):
        return pltpu.make_async_remote_copy(
            src_ref=pslot.at[s],
            dst_ref=pslot.at[s],
            send_sem=p_send.at[to],
            recv_sem=p_recv.at[s],
            device_id=(to, wide),
            device_id_type=MESH,
        )

    @pl.loop(1, SIDE)
    def _(o):
        p_copy(x, (x + o) % SIDE).start()

    def second_slot(d, k):
        return d * 4 + k - 1

    def second_copy(d, k, idx):
        step = 1 if d == 0 else SIDE - 1
        to = (a * p + b * ((q + step) % SIDE)) * 2 + c
        s = second_slot(d, k)
        return pltpu.make_async_remote_copy(
            src_ref=r0.at[idx],
            dst_ref=rc2.at[s],
            send_sem=ring_send,
            recv_sem=rc2_sem.at[s],
            device_id=(x, to),
            device_id_type=MESH,
        )

    def own(j):
        idx = a * p + b * ((q + ring_offset(j)) % SIDE)
        pair_copy(idx).wait_recv()
        first_copy(0, 1, j, idx).wait_recv()
        first_copy(1, 1, j, idx).wait_recv()
        return idx, r0[idx] + g[idx, c] + rc1[slot(0, 1, j)] + rc1[slot(1, 1, j)]

    for j, d, k, more in (
        (0, 0, 4, False), (2, 1, 3, False), (1, 0, 3, True), (4, 1, 2, True),
        (3, 0, 2, True), (6, 1, 1, True), (5, 0, 1, True),
    ):
        idx, value = own(j)
        if more:
            second_copy(d, k + 1, idx).wait_recv()
            value = value + rc2[second_slot(d, k + 1)]
        r0[idx] = value
        second_copy(d, k, idx).start()
    idx, value = own(7)
    for d in range(2):
        second_copy(d, 1, idx).wait_recv()
        value = value + rc2[second_slot(d, 1)]
    down_ref[0] = value[:, :F]
    down_ref[1] = value[:, F:]
    square = jnp.sum((value * value).reshape(PIECE // 8, 8, 2 * F), axis=0)

    def gather(value, buf, mine, count, send, recv, where):
        buf[mine] = value

        def copy(s, to):
            return pltpu.make_async_remote_copy(
                src_ref=buf.at[s],
                dst_ref=buf.at[s],
                send_sem=send.at[to],
                recv_sem=recv.at[s],
                device_id=where(to),
                device_id_type=MESH,
            )

        @pl.loop(1, count)
        def _(o):
            copy(mine, (mine + o) % count).start()

        @pl.loop(1, count)
        def _(o):
            other = (mine + o) % count
            copy(other, other).wait_recv()

        result = jnp.sum(buf[...], axis=0)

        @pl.loop(1, count)
        def _(o):
            copy(mine, (mine + o) % count).wait_send()

        return result

    square = gather(
        square, qxc, x * 2 + c, 2 * SIDE, xc_send, xc_recv,
        lambda to: (to // 2, chip * 2 + to % 2),
    )
    square = gather(
        square, qy, y, SIDE, y_send, y_recv, lambda to: (x, (to * SIDE + z) * 2 + c)
    )
    square = gather(
        square, qz, z, SIDE, z_send, z_recv, lambda to: (x, (y * SIDE + to) * 2 + c)
    )
    lane = lax.broadcasted_iota(jnp.int32, (8, F), 1)
    rms = [jnp.sqrt(jnp.sum(square[:, e * F:(e + 1) * F]) / float(D * FFW)) for e in range(2)]
    rms_ref[...] = jnp.where(lane == 0, rms[0], rms[1])

    @pl.loop(1, SIDE)
    def _(o):
        other = (x + o) % SIDE
        p_copy(other, other).wait_recv()

    pgrad_ref[...] = jnp.sum(pslot[...], axis=0)

    @pl.loop(1, SIDE)
    def _(o):
        p_copy(x, (x + o) % SIDE).wait_send()

    pltpu.make_async_copy(r0, r0, pair_send).wait()
    pltpu.make_async_copy(r0.at[pl.ds(0, 63)], r0.at[pl.ds(0, 63)], ring_send).wait()


def body(upstream, gate_pre, up_pre, down_weight, block_expert, row_token, gate_prob):
    vmem = pl.BlockSpec(memory_space=pltpu.VMEM)
    any_space = pl.BlockSpec(memory_space=pl.ANY)
    dma = pltpu.SemaphoreType.DMA
    down, rms, pgrad, ggrad, ugrad = pl.pallas_call(
        kernel,
        name="experts_backward",
        out_shape=(
            jax.ShapeDtypeStruct((2, PIECE, F), F32),
            jax.ShapeDtypeStruct((8, F), F32),
            jax.ShapeDtypeStruct((8, F), F32),
            jax.ShapeDtypeStruct((ROWS, F), BF16),
            jax.ShapeDtypeStruct((ROWS, F), BF16),
        ),
        in_specs=[
            any_space, any_space, vmem, vmem, vmem, vmem,
            pl.BlockSpec(memory_space=pltpu.SMEM),
        ],
        out_specs=(vmem,) * 5,
        scratch_shapes=[
            pltpu.VMEM((SIDE, ROWS, COLS), BF16),
            pltpu.VMEM((2 * D, F), BF16),
            pltpu.VMEM((64, 2, PIECE, 2 * F), F32),
            pltpu.VMEM((64, PIECE, 2 * F), F32),
            pltpu.VMEM((64, PIECE, 2 * F), F32),
            pltpu.VMEM((8, PIECE, 2 * F), F32),
            pltpu.VMEM((2 * COLS, F), F32),
            pltpu.VMEM((ROWS, 2 * F), F32),
            pltpu.VMEM((ROWS, 2 * F), BF16),
            pltpu.VMEM((NBLK, ROWS, F), BF16),
            pltpu.VMEM((SIDE, 8, F), F32),
            pltpu.VMEM((2 * SIDE, 8, 2 * F), F32),
            pltpu.VMEM((SIDE, 8, 2 * F), F32),
            pltpu.VMEM((SIDE, 8, 2 * F), F32),
            dma((SIDE,)), dma, dma, dma((64,)), dma, dma((64,)), dma((8,)),
            dma((SIDE,)), dma((SIDE,)), dma((2 * SIDE,)), dma((2 * SIDE,)),
            dma((SIDE,)), dma((SIDE,)), dma((SIDE,)), dma((SIDE,)),
        ],
        compiler_params=pltpu.CompilerParams(
            collective_id=0, has_side_effects=True, vmem_limit_bytes=60 * 1024 * 1024
        ),
    )(
        upstream,
        down_weight.reshape(2 * D, F),
        gate_pre,
        up_pre,
        gate_prob.reshape(NBLK, BLOCK),
        row_token.reshape(NBLK, BLOCK),
        block_expert,
    )
    return (
        jnp.transpose(down, (1, 0, 2)),
        rms[0, :2],
        pgrad[:NBLK].reshape(ROWS),
        ggrad,
        ugrad,
    )


def solution(mesh):
    in_specs = (
        P("wide", None),
        P("wide", "blk"),
        P("wide", "blk"),
        P(None, None, "blk"),
        P("wide"),
        P("wide"),
        P("wide"),
    )
    out_specs = (P("wide", None, "blk"), P(), P("wide"), P("wide", "blk"), P("wide", "blk"))
    return jax.shard_map(body, mesh=mesh, in_specs=in_specs, out_specs=out_specs, check_vma=False)
```

```python
import functools

import jax
import jax.numpy as jnp
from jax import lax
from jax.experimental import pallas as pl
from jax.experimental.pallas import tpu as pltpu
from jax.sharding import PartitionSpec as P

D = 7168
FFW = 1024
BLOCK = 128
ROWS = 384
NBLK = 3
F = 128
SIDE = 8
PIECE = 56
COLS = 896
F32 = jnp.float32
BF16 = jnp.bfloat16
VMEM_LIMIT = 60
MESH = pl.DeviceIdType.MESH


def ring_offset(j):
    far = 4 - (j + 1) // 2
    odd = j % 2
    return (odd * far + (1 - odd) * (8 - far)) % 8


def across(row):
    return jnp.transpose(jnp.broadcast_to(row, (F, F)))


def kernel(
    u_hbm, w_hbm, gate_hbm, up_hbm, prob_hbm, tok_hbm, expert_hbm,
    down_ref, rms_ref, pgrad_ref, ggrad_ref, ugrad_ref,
    gate_ref, up_ref, prob_ref, tok_ref, expert_ref,
    ub, wv, g, r0, rc1, rc2, wf, pacc, wp, oh, pslot, qxc, qy, qz,
    insem, usem, wsem, pair_send, r0_sem, ring_send, rc1_sem, rc2_sem,
    p_send, p_recv, xc_send, xc_recv, y_send, y_recv, z_send, z_recv,
):
    x = lax.axis_index("blk")
    wide = lax.axis_index("wide")
    c = wide % 2
    chip = wide // 2
    y = chip // SIDE
    z = chip % SIDE
    p = (1 - c) * y + c * z
    q = (1 - c) * z + c * y
    a = 8 - 7 * c
    b = 1 + 7 * c

    small = [
        pltpu.make_async_copy(src, dst, insem.at[n])
        for n, (src, dst) in enumerate((
            (tok_hbm, tok_ref), (prob_hbm, prob_ref), (expert_hbm, expert_ref),
            (gate_hbm, gate_ref), (up_hbm, up_ref),
        ))
    ]
    for copy in small:
        copy.start()

    def block_copy(i):
        yi = (y + ring_offset(i)) % SIDE
        cols = pl.ds(pl.multiple_of(yi * COLS, 128), COLS)
        return pltpu.make_async_copy(u_hbm.at[:, cols], ub.at[i], usem.at[i])

    @pl.loop(0, SIDE)
    def _(i):
        block_copy(i).start()

    w_copy = pltpu.make_async_copy(w_hbm, wv, wsem)
    w_copy.start()

    barrier = pltpu.get_barrier_semaphore()

    def greet(xi, wi):
        pl.semaphore_signal(barrier, inc=1, device_id=(xi, wi), device_id_type=MESH)

    @pl.loop(1, SIDE)
    def _(o):
        greet((x + o) % SIDE, wide)
        greet((x + o) % SIDE, chip * 2 + 1 - c)
        greet(x, (((y + o) % SIDE) * SIDE + z) * 2 + c)
        greet(x, (y * SIDE + (z + o) % SIDE) * 2 + c)

    greet(x, chip * 2 + 1 - c)

    for copy in small:
        copy.wait()

    total = jnp.zeros((ROWS, 2 * F), F32)
    token_iota = lax.broadcasted_iota(jnp.int32, (ROWS, F), 0)
    for k in range(NBLK):
        rows = pl.ds(k * BLOCK, BLOCK)
        gate = gate_ref[rows, :].astype(F32)
        up = up_ref[rows, :].astype(F32)
        hidden = gate * jax.nn.sigmoid(gate) * up
        weighted = (hidden * across(prob_ref[pl.ds(k, 1), :])).astype(BF16).astype(F32)
        expert = jnp.full((F, F), expert_ref[k], jnp.int32)
        both = jnp.concatenate(
            [jnp.where(expert == e, weighted, 0.0) for e in range(2)], axis=1
        ).astype(BF16)
        hot = jnp.where(token_iota == tok_ref[pl.ds(k, 1), :], 1.0, 0.0).astype(BF16)
        oh[k] = hot
        total = total + jnp.dot(hot, both, preferred_element_type=F32)
    wp[...] = total.astype(BF16)

    @pl.loop(0, SIDE)
    def _(i):
        block_copy(i).wait()
        yi = (y + ring_offset(i)) % SIDE
        value = lax.dot_general(
            ub[i], wp[...], (((0,), (0,)), ((), ())), preferred_element_type=F32
        )
        g[pl.ds(yi * SIDE, SIDE)] = value.reshape(SIDE, 2, PIECE, 2 * F)

    pl.semaphore_wait(barrier, 4 * (SIDE - 1) + 1)

    def pair_copy(r, j, sem):
        far, near = (other_p + ring_offset(r)) % SIDE, (other_q + ring_offset(j)) % SIDE
        idx = b * far + a * near
        return pltpu.make_async_remote_copy(
            src_ref=g.at[idx, 1 - c],
            dst_ref=r0.at[idx],
            send_sem=pair_send,
            recv_sem=r0_sem.at[sem],
            device_id=(x, chip * 2 + 1 - c),
            device_id_type=MESH,
        )

    other_p, other_q = q, p

    @pl.loop(0, SIDE)
    def _(j):
        pair_copy(0, j, j).start()

    @pl.loop(1, SIDE)
    def _(r):
        @pl.loop(0, SIDE)
        def _(j):
            pair_copy(r, j, SIDE - 1 + r).start()

    def pair_wait(sem, pieces):
        part = r0.at[pl.ds(0, pieces)]
        pltpu.make_async_copy(part, part, r0_sem.at[sem]).wait()

    def slot(d, k, j):
        return 6 * SIDE + j if k == 4 else (d * 3 + k - 1) * SIDE + j

    def first_copy(d, k, j, idx):
        step = 1 if d == 0 else SIDE - 1
        to = (a * ((p + step) % SIDE) + b * q) * 2 + c
        s = slot(d, k, j)
        return pltpu.make_async_remote_copy(
            src_ref=r0.at[idx],
            dst_ref=rc1.at[s],
            send_sem=ring_send,
            recv_sem=rc1_sem.at[s],
            device_id=(x, to),
            device_id_type=MESH,
        )

    def first_send(d, k, j, more):
        step = 1 if d == 0 else SIDE - 1
        idx = a * ((p + step * k) % SIDE) + b * ((q + ring_offset(j)) % SIDE)
        if k == 4:
            pair_wait(j, 1)
        value = r0[idx] + g[idx, c]
        if more:
            first_copy(d, k + 1, j, idx).wait_recv()
            value = value + rc1[slot(d, k + 1, j)]
        r0[idx] = value
        first_copy(d, k, j, idx).start()

    def project(i):
        yi = (y + ring_offset(i)) % SIDE
        wf[...] = wv[pl.ds(pl.multiple_of(yi * 2 * COLS, 16), 2 * COLS), :].astype(F32)
        weight = jnp.concatenate(
            [wf[pl.ds(e, COLS, stride=2), :].astype(BF16) for e in range(2)], axis=1
        )
        pacc[...] += jnp.dot(ub[i], weight, preferred_element_type=F32)

    @pl.loop(0, 4)
    def _(j):
        first_send(0, 4, j + 4, False)
        first_send(1, 4, j, False)

    pair_wait(SIDE, SIDE)
    pair_wait(SIDE + 1, SIDE)

    @pl.loop(0, 4)
    def _(j):
        first_send(0, 3, j, False)
        first_send(1, 3, j + 4, False)

    w_copy.wait()
    pacc[...] = jnp.zeros_like(pacc)

    @pl.loop(0, 4)
    def _(j):
        first_send(0, 3, j + 4, True)
        first_send(1, 3, j, True)
        project(j)

    pair_wait(SIDE + 2, SIDE)
    pair_wait(SIDE + 3, SIDE)

    @pl.loop(0, 4)
    def _(j):
        for h in range(2):
            first_send(0, 2, 2 * j + h, True)
            first_send(1, 2, (2 * j + h + 4) % SIDE, True)
        project(j + 4)

    def exchange(buf, mine, count, send, recv, where):
        @pl.loop(1, count)
        def _(o):
            pltpu.make_async_remote_copy(
                src_ref=buf.at[mine],
                dst_ref=buf.at[mine],
                send_sem=send,
                recv_sem=recv,
                device_id=where((mine + o) % count),
                device_id_type=MESH,
            ).start()

    def exchanged(buf, count, sem):
        part = buf.at[pl.ds(0, count - 1)]
        pltpu.make_async_copy(part, part, sem).wait()

    high = pacc[...].astype(BF16)
    rest = pacc[...] - high.astype(F32)
    middle = rest.astype(BF16)
    low = (rest - middle.astype(F32)).astype(BF16)
    pslot[x] = jnp.zeros((8, F), F32)
    for k in range(NBLK):
        rows = pl.ds(k * BLOCK, BLOCK)
        hot = oh[k]
        moved = sum(
            lax.dot_general(hot, term, (((0,), (0,)), ((), ())), preferred_element_type=F32)
            for term in (low, middle, high)
        )
        expert = jnp.full((F, F), expert_ref[k], jnp.int32)
        projected = jnp.where(expert == 0, moved[:, :F], moved[:, F:])
        gate = gate_ref[rows, :].astype(F32)
        up = up_ref[rows, :].astype(F32)
        sig = jax.nn.sigmoid(gate)
        active = gate * sig
        scaled = across(prob_ref[pl.ds(k, 1), :]) * projected
        ugrad_ref[rows, :] = (scaled * active).astype(BF16)
        ggrad_ref[rows, :] = (scaled * up * sig * (1.0 + gate * (1.0 - sig))).astype(BF16)
        part = jnp.transpose(active * up * projected)
        pslot[x, pl.ds(k, 1), :] = jnp.sum(part, axis=0, keepdims=True)

    exchange(pslot, x, SIDE, p_send, p_recv, lambda to: (to, wide))

    pair_wait(SIDE + 4, SIDE)
    pair_wait(SIDE + 5, SIDE)

    @pl.loop(0, SIDE)
    def _(j):
        first_send(0, 1, j, True)
        first_send(1, 1, j, True)

    pair_wait(SIDE + 6, SIDE)

    def second_slot(d, k):
        return d * 4 + k - 1

    def second_copy(d, k, idx):
        step = 1 if d == 0 else SIDE - 1
        to = (a * p + b * ((q + step) % SIDE)) * 2 + c
        s = second_slot(d, k)
        return pltpu.make_async_remote_copy(
            src_ref=r0.at[idx],
            dst_ref=rc2.at[s],
            send_sem=ring_send,
            recv_sem=rc2_sem.at[s],
            device_id=(x, to),
            device_id_type=MESH,
        )

    def own(j):
        idx = a * p + b * ((q + ring_offset(j)) % SIDE)
        first_copy(0, 1, j, idx).wait_recv()
        first_copy(1, 1, j, idx).wait_recv()
        return idx, r0[idx] + g[idx, c] + rc1[slot(0, 1, j)] + rc1[slot(1, 1, j)]

    for j, d, k, more in (
        (0, 0, 4, False), (2, 1, 3, False), (1, 0, 3, True), (4, 1, 2, True),
        (3, 0, 2, True), (6, 1, 1, True), (5, 0, 1, True),
    ):
        idx, value = own(j)
        if more:
            second_copy(d, k + 1, idx).wait_recv()
            value = value + rc2[second_slot(d, k + 1)]
        r0[idx] = value
        second_copy(d, k, idx).start()
    idx, value = own(7)
    for d in range(2):
        second_copy(d, 1, idx).wait_recv()
        value = value + rc2[second_slot(d, 1)]
    down_ref[0] = value[:, :F]
    down_ref[1] = value[:, F:]
    column = jnp.sum(value * value, axis=0, keepdims=True)
    square = jnp.concatenate([column[:, :F], column[:, F:]], axis=0)

    stages = (
        (qxc, x * 2 + c, 2 * SIDE, xc_send, xc_recv, lambda to: (to // 2, chip * 2 + to % 2)),
        (qy, y, SIDE, y_send, y_recv, lambda to: (x, (to * SIDE + z) * 2 + c)),
        (qz, z, SIDE, z_send, z_recv, lambda to: (x, (y * SIDE + to) * 2 + c)),
    )
    for buf, mine, count, send, recv, where in stages:
        buf[mine] = square
        exchange(buf, mine, count, send, recv, where)
        exchanged(buf, count, recv)
        square = jnp.sum(buf[...], axis=0)
    mean = jnp.sum(square, axis=1, keepdims=True) / float(D * FFW)
    rms_ref[...] = jnp.broadcast_to(jnp.sqrt(mean), (2, F))

    exchanged(pslot, SIDE, p_recv)
    pgrad_ref[...] = jnp.sum(pslot[...], axis=0)

    exchanged(pslot, SIDE, p_send)
    for buf, _, count, send, _, _ in stages:
        exchanged(buf, count, send)
    pltpu.make_async_copy(r0, r0, pair_send).wait()
    pltpu.make_async_copy(r0.at[pl.ds(0, 63)], r0.at[pl.ds(0, 63)], ring_send).wait()


def place(down_ref, rms_ref, pgrad_ref, ggrad_ref, ugrad_ref, down, rms, pgrad, ggrad, ugrad):
    for e in range(2):
        down[:, e, :] = down_ref[e]
    lane = lax.broadcasted_iota(jnp.int32, (1, F), 1)
    rms[...] = jnp.where(lane == 0, rms_ref[0:1, :], rms_ref[1:2, :])[:, :2]
    pgrad[...] = pgrad_ref[0:NBLK, :]
    ggrad[...] = ggrad_ref[...]
    ugrad[...] = ugrad_ref[...]


def body(upstream, gate_pre, up_pre, down_weight, block_expert, row_token, gate_prob):
    vmem = pl.BlockSpec(memory_space=pltpu.VMEM)
    hbm = pl.BlockSpec(memory_space=pl.ANY)
    dma = pltpu.SemaphoreType.DMA
    results = pl.pallas_call(
        kernel,
        name="experts_backward",
        out_shape=(
            jax.ShapeDtypeStruct((2, PIECE, F), F32),
            jax.ShapeDtypeStruct((2, F), F32),
            jax.ShapeDtypeStruct((8, F), F32),
            jax.ShapeDtypeStruct((ROWS, F), BF16),
            jax.ShapeDtypeStruct((ROWS, F), BF16),
        ),
        in_specs=[hbm] * 7,
        out_specs=(vmem,) * 5,
        scratch_shapes=[
            pltpu.VMEM((ROWS, F), BF16),
            pltpu.VMEM((ROWS, F), BF16),
            pltpu.VMEM((NBLK, BLOCK), F32),
            pltpu.VMEM((NBLK, BLOCK), jnp.int32),
            pltpu.SMEM((NBLK,), jnp.int32),
            pltpu.VMEM((SIDE, ROWS, COLS), BF16),
            pltpu.VMEM((2 * D, F), BF16),
            pltpu.VMEM((64, 2, PIECE, 2 * F), F32),
            pltpu.VMEM((64, PIECE, 2 * F), F32),
            pltpu.VMEM((56, PIECE, 2 * F), F32),
            pltpu.VMEM((8, PIECE, 2 * F), F32),
            pltpu.VMEM((2 * COLS, F), F32),
            pltpu.VMEM((ROWS, 2 * F), F32),
            pltpu.VMEM((ROWS, 2 * F), BF16),
            pltpu.VMEM((NBLK, ROWS, F), BF16),
            pltpu.VMEM((SIDE, 8, F), F32),
            pltpu.VMEM((2 * SIDE, 2, F), F32),
            pltpu.VMEM((SIDE, 2, F), F32),
            pltpu.VMEM((SIDE, 2, F), F32),
            dma((5,)), dma((SIDE,)), dma, dma, dma((2 * SIDE - 1,)), dma, dma((56,)), dma((8,)),
            dma, dma, dma, dma, dma, dma, dma, dma,
        ],
        compiler_params=pltpu.CompilerParams(
            collective_id=0, has_side_effects=True, vmem_limit_bytes=VMEM_LIMIT * 1024 * 1024
        ),
    )(
        upstream,
        down_weight.reshape(2 * D, F),
        gate_pre,
        up_pre,
        gate_prob.reshape(NBLK, BLOCK),
        row_token.reshape(NBLK, BLOCK),
        block_expert,
    )
    down, rms, pgrad, ggrad, ugrad = pl.pallas_call(
        place,
        name="place_results",
        out_shape=(
            jax.ShapeDtypeStruct((PIECE, 2, F), F32),
            jax.ShapeDtypeStruct((1, 2), F32),
            jax.ShapeDtypeStruct((NBLK, BLOCK), F32),
            jax.ShapeDtypeStruct((ROWS, F), BF16),
            jax.ShapeDtypeStruct((ROWS, F), BF16),
        ),
        in_specs=[vmem] * 5,
        out_specs=(vmem,) * 5,
    )(*results)
    return down, rms.reshape(2), pgrad.reshape(ROWS), ggrad, ugrad


def solution(mesh):
    in_specs = (
        P("wide", None),
        P("wide", "blk"),
        P("wide", "blk"),
        P(None, None, "blk"),
        P("wide"),
        P("wide"),
        P("wide"),
    )
    out_specs = (P("wide", None, "blk"), P(), P("wide"), P("wide", "blk"), P("wide", "blk"))
    return jax.shard_map(body, mesh=mesh, in_specs=in_specs, out_specs=out_specs, check_vma=False)
```

```python
import functools

import jax
import jax.numpy as jnp
from jax import lax
from jax.experimental import pallas as pl
from jax.experimental.pallas import tpu as pltpu
from jax.sharding import PartitionSpec as P

D = 7168
FFW = 1024
BLOCK = 128
ROWS = 384
NBLK = 3
F = 128
SIDE = 8
PIECE = 56
COLS = 896
F32 = jnp.float32
BF16 = jnp.bfloat16
VMEM_LIMIT = 60
MESH = pl.DeviceIdType.MESH


def ring_offset(j):
    far = 4 - (j + 1) // 2
    odd = j % 2
    return (odd * far + (1 - odd) * (8 - far)) % 8


def ring_from(at):
    return lambda t: (at + ring_offset(t)) % SIDE


def starts_plus(j):
    return ((j + 3) % SIDE) // 4


def across(row):
    return jnp.transpose(jnp.broadcast_to(row, (F, F)))


def kernel(
    u_hbm, w_hbm, gate_hbm, up_hbm, prob_hbm, tok_hbm, expert_hbm,
    down_ref, rms_ref, pgrad_ref, ggrad_ref, ugrad_ref,
    gate_ref, up_ref, prob_ref, tok_ref, expert_ref,
    ub, wv, g, r0, rc1, rc2, wf, pacc, wp, oh, pslot, qxc, qy, qz,
    insem, usem, wsem, pair_send, r0_sem, ring_send, rc1_sem, rc2_sem,
    p_send, p_recv, xc_send, xc_recv, y_send, y_recv, z_send, z_recv,
):
    x = lax.axis_index("blk")
    wide = lax.axis_index("wide")
    c = wide % 2
    chip = wide // 2
    y = chip // SIDE
    z = chip % SIDE
    p = (1 - c) * y + c * z
    q = (1 - c) * z + c * y
    a = 8 - 7 * c
    b = 1 + 7 * c

    small = [
        pltpu.make_async_copy(src, dst, insem.at[n])
        for n, (src, dst) in enumerate((
            (tok_hbm, tok_ref), (prob_hbm, prob_ref), (expert_hbm, expert_ref),
            (gate_hbm, gate_ref), (up_hbm, up_ref),
        ))
    ]
    for copy in small:
        copy.start()

    def block_copy(i):
        yi = (y + ring_offset(i)) % SIDE
        cols = pl.ds(pl.multiple_of(yi * COLS, 128), COLS)
        return pltpu.make_async_copy(u_hbm.at[:, cols], ub.at[i], usem.at[i])

    @pl.loop(0, SIDE)
    def _(i):
        block_copy(i).start()

    w_copy = pltpu.make_async_copy(w_hbm, wv, wsem)
    w_copy.start()

    barrier = pltpu.get_barrier_semaphore()

    def greet(xi, wi):
        pl.semaphore_signal(barrier, inc=1, device_id=(xi, wi), device_id_type=MESH)

    @pl.loop(1, SIDE)
    def _(o):
        greet((x + o) % SIDE, wide)
        greet((x + o) % SIDE, chip * 2 + 1 - c)
        greet(x, (((y + o) % SIDE) * SIDE + z) * 2 + c)
        greet(x, (y * SIDE + (z + o) % SIDE) * 2 + c)

    greet(x, chip * 2 + 1 - c)

    for copy in small:
        copy.wait()

    total = jnp.zeros((ROWS, 2 * F), F32)
    token_iota = lax.broadcasted_iota(jnp.int32, (ROWS, F), 0)
    for k in range(NBLK):
        rows = pl.ds(k * BLOCK, BLOCK)
        gate = gate_ref[rows, :].astype(F32)
        up = up_ref[rows, :].astype(F32)
        hidden = gate * jax.nn.sigmoid(gate) * up
        weighted = (hidden * across(prob_ref[pl.ds(k, 1), :])).astype(BF16).astype(F32)
        expert = jnp.full((F, F), expert_ref[k], jnp.int32)
        both = jnp.concatenate(
            [jnp.where(expert == e, weighted, 0.0) for e in range(2)], axis=1
        ).astype(BF16)
        hot = jnp.where(token_iota == tok_ref[pl.ds(k, 1), :], 1.0, 0.0).astype(BF16)
        oh[k] = hot
        total = total + jnp.dot(hot, both, preferred_element_type=F32)
    wp[...] = total.astype(BF16)

    def gradient(i):
        block_copy(i).wait()
        yi = (y + ring_offset(i)) % SIDE
        value = lax.dot_general(
            ub[i], wp[...], (((0,), (0,)), ((), ())), preferred_element_type=F32
        )
        g[pl.ds(yi * SIDE, SIDE)] = value.reshape(SIDE, 2, PIECE, 2 * F)

    @pl.loop(0, 3)
    def _(i):
        gradient(i)

    pl.semaphore_wait(barrier, 4 * (SIDE - 1) + 1)

    def pair_copy(r, j, sem):
        far, near = (other_p + ring_offset(r)) % SIDE, (other_q + ring_offset(j)) % SIDE
        idx = b * far + a * near
        return pltpu.make_async_remote_copy(
            src_ref=g.at[idx, 1 - c],
            dst_ref=r0.at[idx],
            send_sem=pair_send,
            recv_sem=r0_sem.at[sem],
            device_id=(x, chip * 2 + 1 - c),
            device_id_type=MESH,
        )

    other_p, other_q = q, p

    def pair_lead(j):
        pair_copy(0, j, j).start()
        pair_copy(1 + starts_plus(j), j, SIDE + j).start()

    def pair_rest(j):
        pair_copy(2 - starts_plus(j), j, 2 * SIDE).start()

    def pair_group(r):
        @pl.loop(0, SIDE)
        def _(j):
            pair_copy(r, j, 2 * SIDE - 2 + r).start()

    def pair_wait(sem, pieces):
        part = r0.at[pl.ds(0, pieces)]
        pltpu.make_async_copy(part, part, r0_sem.at[sem]).wait()

    def slot(d, k, j):
        return 6 * SIDE + j if k == 4 else (d * 3 + k - 1) * SIDE + j

    def ring_copy(d, s, idx):
        step = 1 if d == 0 else SIDE - 1
        to = (a * ((p + step) % SIDE) + b * q) * 2 + c
        return pltpu.make_async_remote_copy(
            src_ref=r0.at[idx],
            dst_ref=rc1.at[s],
            send_sem=ring_send,
            recv_sem=rc1_sem.at[s],
            device_id=(x, to),
            device_id_type=MESH,
        )

    def first_copy(d, k, j, idx):
        return ring_copy(d, slot(d, k, j), idx)

    def lead_send(j):
        m = starts_plus(j)
        near = b * ((q + ring_offset(j)) % SIDE)
        pair_wait(j, 1)
        pair_wait(SIDE + j, 1)
        for d, far, s in (
            (0, p + 3 + m, m * slot(0, 4, j) + (1 - m) * slot(0, 3, j)),
            (1, p + 4 + m, (1 - m) * slot(1, 4, j) + m * slot(1, 3, j)),
        ):
            idx = a * (far % SIDE) + near
            r0[idx] = r0[idx] + g[idx, c]
            ring_copy(d, s, idx).start()

    def first_send(d, k, j):
        step = 1 if d == 0 else SIDE - 1
        idx = a * ((p + step * k) % SIDE) + b * ((q + ring_offset(j)) % SIDE)
        first_copy(d, k + 1, j, idx).wait_recv()
        r0[idx] = r0[idx] + g[idx, c] + rc1[slot(d, k + 1, j)]
        first_copy(d, k, j, idx).start()

    def project(i):
        yi = (y + ring_offset(i)) % SIDE
        wf[...] = wv[pl.ds(pl.multiple_of(yi * 2 * COLS, 16), 2 * COLS), :].astype(F32)
        weight = jnp.concatenate(
            [wf[pl.ds(e, COLS, stride=2), :].astype(BF16) for e in range(2)], axis=1
        )
        pacc[...] += jnp.dot(ub[i], weight, preferred_element_type=F32)

    pair_lead(0)
    pair_lead(1)

    @pl.loop(3, SIDE)
    def _(i):
        gradient(i)
        pair_lead(i - 1)
        pair_rest(i - 3)

        @pl.when(i >= 4)
        def _():
            lead_send(i - 4)

    pair_lead(7)
    lead_send(4)

    @pl.loop(5, SIDE)
    def _(j):
        pair_rest(j)

    pair_group(3)
    lead_send(5)
    pair_group(4)
    lead_send(6)
    lead_send(7)

    @pl.loop(5, SIDE)
    def _(r):
        pair_group(r)

    w_copy.wait()
    pacc[...] = jnp.zeros_like(pacc)

    def exchange(buf, mine, count, send, recv, order, where):
        @pl.loop(0, count - 1)
        def _(t):
            pltpu.make_async_remote_copy(
                src_ref=buf.at[mine],
                dst_ref=buf.at[mine],
                send_sem=send,
                recv_sem=recv,
                device_id=where(order(t)),
                device_id_type=MESH,
            ).start()

    def exchanged(buf, count, sem):
        part = buf.at[pl.ds(0, count - 1)]
        pltpu.make_async_copy(part, part, sem).wait()

    def rows_back():
        high = pacc[...].astype(BF16)
        rest = pacc[...] - high.astype(F32)
        middle = rest.astype(BF16)
        low = (rest - middle.astype(F32)).astype(BF16)
        pslot[x] = jnp.zeros((8, F), F32)
        for k in range(NBLK):
            rows = pl.ds(k * BLOCK, BLOCK)
            hot = oh[k]
            moved = sum(
                lax.dot_general(hot, term, (((0,), (0,)), ((), ())), preferred_element_type=F32)
                for term in (low, middle, high)
            )
            expert = jnp.full((F, F), expert_ref[k], jnp.int32)
            projected = jnp.where(expert == 0, moved[:, :F], moved[:, F:])
            gate = gate_ref[rows, :].astype(F32)
            up = up_ref[rows, :].astype(F32)
            sig = jax.nn.sigmoid(gate)
            active = gate * sig
            scaled = across(prob_ref[pl.ds(k, 1), :]) * projected
            ugrad_ref[rows, :] = (scaled * active).astype(BF16)
            ggrad_ref[rows, :] = (scaled * up * sig * (1.0 + gate * (1.0 - sig))).astype(BF16)
            part = jnp.transpose(active * up * projected)
            pslot[x, pl.ds(k, 1), :] = jnp.sum(part, axis=0, keepdims=True)

        exchange(pslot, x, SIDE, p_send, p_recv, ring_from(x), lambda to: (to, wide))

    def second_slot(d, k):
        return d * 4 + k - 1

    def second_copy(d, k, idx):
        step = 1 if d == 0 else SIDE - 1
        to = (a * p + b * ((q + step) % SIDE)) * 2 + c
        s = second_slot(d, k)
        return pltpu.make_async_remote_copy(
            src_ref=r0.at[idx],
            dst_ref=rc2.at[s],
            send_sem=ring_send,
            recv_sem=rc2_sem.at[s],
            device_id=(x, to),
            device_id_type=MESH,
        )

    def own(j):
        idx = a * p + b * ((q + ring_offset(j)) % SIDE)
        first_copy(0, 1, j, idx).wait_recv()
        first_copy(1, 1, j, idx).wait_recv()
        return idx, r0[idx] + g[idx, c] + rc1[slot(0, 1, j)] + rc1[slot(1, 1, j)]

    def second_send(j, d, k):
        idx, value = own(j)
        if (d, k) not in ((0, 4), (1, 3)):
            second_copy(d, k + 1, idx).wait_recv()
            value = value + rc2[second_slot(d, k + 1)]
        r0[idx] = value
        second_copy(d, k, idx).start()

    plus = (
        (2, 0), (3, 2), (3, 1), (3, 4), (1, 0), (2, 2), (2, 1), (2, 4), (3, 3), (1, 2),
        (1, 1), (1, 4), (2, 3), (2, 6), (2, 5), (2, 7), (1, 3), (1, 6), (1, 5), (1, 7),
    )
    minus = (
        (3, 0), (2, 2), (2, 1), (2, 4), (2, 0), (1, 2), (1, 1), (1, 4), (1, 0), (2, 3),
        (3, 6), (3, 5), (3, 7), (1, 3), (2, 6), (2, 5), (2, 7), (1, 6), (1, 5), (1, 7),
    )
    for n in range(len(plus)):
        if n == 0:
            for r in (2, 3, 4):
                pair_wait(2 * SIDE - 2 + r, SIDE)
        if n == 4:
            for r in (5, 6):
                pair_wait(2 * SIDE - 2 + r, SIDE)
        first_send(0, *plus[n])
        first_send(1, *minus[n])
        if n in (0, 2, 4, 6):
            @pl.loop(n, n + 2)
            def _(i):
                project(i)
        if n == 8:
            rows_back()
        if n == 14:
            pair_wait(3 * SIDE - 3, SIDE)
            second_send(0, 0, 4)
        if n == 15:
            second_send(2, 1, 3)
        if n == 16:
            second_send(1, 0, 3)
        if n == 18:
            second_send(4, 1, 2)
    second_send(3, 0, 2)
    second_send(6, 1, 1)
    second_send(5, 0, 1)
    idx, value = own(7)
    for d in range(2):
        second_copy(d, 1, idx).wait_recv()
        value = value + rc2[second_slot(d, 1)]
    down_ref[0] = value[:, :F]
    down_ref[1] = value[:, F:]
    column = jnp.sum(value * value, axis=0, keepdims=True)
    square = jnp.concatenate([column[:, :F], column[:, F:]], axis=0)

    stages = (
        (
            qxc, x * 2 + c, 2 * SIDE, xc_send, xc_recv,
            lambda t: ((x + ring_offset(t // 2)) % SIDE) * 2 + (c + 1 + t) % 2,
            lambda to: (to // 2, chip * 2 + to % 2),
        ),
        (
            qy, y, SIDE, y_send, y_recv, ring_from(y),
            lambda to: (x, (to * SIDE + z) * 2 + c),
        ),
        (
            qz, z, SIDE, z_send, z_recv, ring_from(z),
            lambda to: (x, (y * SIDE + to) * 2 + c),
        ),
    )
    for buf, mine, count, send, recv, order, where in stages:
        buf[mine] = square
        exchange(buf, mine, count, send, recv, order, where)
        exchanged(buf, count, recv)
        square = jnp.sum(buf[...], axis=0)
    mean = jnp.sum(square, axis=1, keepdims=True) / float(D * FFW)
    rms_ref[...] = jnp.broadcast_to(jnp.sqrt(mean), (2, F))

    exchanged(pslot, SIDE, p_recv)
    pgrad_ref[...] = jnp.sum(pslot[...], axis=0)

    exchanged(pslot, SIDE, p_send)
    for buf, _, count, send, _, _, _ in stages:
        exchanged(buf, count, send)
    pltpu.make_async_copy(r0, r0, pair_send).wait()
    pltpu.make_async_copy(r0.at[pl.ds(0, 63)], r0.at[pl.ds(0, 63)], ring_send).wait()


def place(down_ref, rms_ref, pgrad_ref, ggrad_ref, ugrad_ref, down, rms, pgrad, ggrad, ugrad):
    for e in range(2):
        down[:, e, :] = down_ref[e]
    lane = lax.broadcasted_iota(jnp.int32, (1, F), 1)
    rms[...] = jnp.where(lane == 0, rms_ref[0:1, :], rms_ref[1:2, :])[:, :2]
    pgrad[...] = pgrad_ref[0:NBLK, :]
    ggrad[...] = ggrad_ref[...]
    ugrad[...] = ugrad_ref[...]


def body(upstream, gate_pre, up_pre, down_weight, block_expert, row_token, gate_prob):
    vmem = pl.BlockSpec(memory_space=pltpu.VMEM)
    hbm = pl.BlockSpec(memory_space=pl.ANY)
    dma = pltpu.SemaphoreType.DMA
    results = pl.pallas_call(
        kernel,
        name="experts_backward",
        out_shape=(
            jax.ShapeDtypeStruct((2, PIECE, F), F32),
            jax.ShapeDtypeStruct((2, F), F32),
            jax.ShapeDtypeStruct((8, F), F32),
            jax.ShapeDtypeStruct((ROWS, F), BF16),
            jax.ShapeDtypeStruct((ROWS, F), BF16),
        ),
        in_specs=[hbm] * 7,
        out_specs=(vmem,) * 5,
        scratch_shapes=[
            pltpu.VMEM((ROWS, F), BF16),
            pltpu.VMEM((ROWS, F), BF16),
            pltpu.VMEM((NBLK, BLOCK), F32),
            pltpu.VMEM((NBLK, BLOCK), jnp.int32),
            pltpu.SMEM((NBLK,), jnp.int32),
            pltpu.VMEM((SIDE, ROWS, COLS), BF16),
            pltpu.VMEM((2 * D, F), BF16),
            pltpu.VMEM((64, 2, PIECE, 2 * F), F32),
            pltpu.VMEM((64, PIECE, 2 * F), F32),
            pltpu.VMEM((56, PIECE, 2 * F), F32),
            pltpu.VMEM((8, PIECE, 2 * F), F32),
            pltpu.VMEM((2 * COLS, F), F32),
            pltpu.VMEM((ROWS, 2 * F), F32),
            pltpu.VMEM((ROWS, 2 * F), BF16),
            pltpu.VMEM((NBLK, ROWS, F), BF16),
            pltpu.VMEM((SIDE, 8, F), F32),
            pltpu.VMEM((2 * SIDE, 2, F), F32),
            pltpu.VMEM((SIDE, 2, F), F32),
            pltpu.VMEM((SIDE, 2, F), F32),
            dma((5,)), dma((SIDE,)), dma, dma, dma((3 * SIDE - 2,)), dma, dma((56,)), dma((8,)),
            dma, dma, dma, dma, dma, dma, dma, dma,
        ],
        compiler_params=pltpu.CompilerParams(
            collective_id=0, has_side_effects=True, vmem_limit_bytes=VMEM_LIMIT * 1024 * 1024
        ),
    )(
        upstream,
        down_weight.reshape(2 * D, F),
        gate_pre,
        up_pre,
        gate_prob.reshape(NBLK, BLOCK),
        row_token.reshape(NBLK, BLOCK),
        block_expert,
    )
    down, rms, pgrad, ggrad, ugrad = pl.pallas_call(
        place,
        name="place_results",
        out_shape=(
            jax.ShapeDtypeStruct((PIECE, 2, F), F32),
            jax.ShapeDtypeStruct((1, 2), F32),
            jax.ShapeDtypeStruct((NBLK, BLOCK), F32),
            jax.ShapeDtypeStruct((ROWS, F), BF16),
            jax.ShapeDtypeStruct((ROWS, F), BF16),
        ),
        in_specs=[vmem] * 5,
        out_specs=(vmem,) * 5,
    )(*results)
    return down, rms.reshape(2), pgrad.reshape(ROWS), ggrad, ugrad


def solution(mesh):
    in_specs = (
        P("wide", None),
        P("wide", "blk"),
        P("wide", "blk"),
        P(None, None, "blk"),
        P("wide"),
        P("wide"),
        P("wide"),
    )
    out_specs = (P("wide", None, "blk"), P(), P("wide"), P("wide", "blk"), P("wide", "blk"))
    return jax.shard_map(body, mesh=mesh, in_specs=in_specs, out_specs=out_specs, check_vma=False)
```

```python
import functools

import jax
import jax.numpy as jnp
from jax import lax
from jax.experimental import pallas as pl
from jax.experimental.pallas import tpu as pltpu
from jax.sharding import PartitionSpec as P

D = 7168
FFW = 1024
BLOCK = 128
ROWS = 384
NBLK = 3
F = 128
SIDE = 8
PIECE = 56
COLS = 896
F32 = jnp.float32
BF16 = jnp.bfloat16
VMEM_LIMIT = 60
MESH = pl.DeviceIdType.MESH


def ring_offset(j):
    far = 4 - (j + 1) // 2
    odd = j % 2
    return (odd * far + (1 - odd) * (8 - far)) % 8


def ring_from(at):
    return lambda t: (at + ring_offset(t)) % SIDE


def starts_plus(j):
    return ((j + 3) % SIDE) // 4


def across(row):
    return jnp.transpose(jnp.broadcast_to(row, (F, F)))


def kernel(
    u_hbm, w_hbm, gate_hbm, up_hbm, prob_hbm, tok_hbm, expert_hbm,
    down_ref, rms_ref, pgrad_ref, ggrad_ref, ugrad_ref,
    gate_ref, up_ref, prob_ref, tok_ref, expert_ref,
    ub, wv, g, r0, rc1, rc2, wf, pacc, wp, oh, pslot, qxc, qy, qz,
    insem, usem, wsem, pair_send, r0_sem, ring_send, rc1_sem, rc2_sem,
    p_send, p_recv, xc_send, xc_recv, y_send, y_recv, z_send, z_recv,
):
    x = lax.axis_index("blk")
    wide = lax.axis_index("wide")
    c = wide % 2
    chip = wide // 2
    y = chip // SIDE
    z = chip % SIDE
    p = (1 - c) * y + c * z
    q = (1 - c) * z + c * y
    a = 8 - 7 * c
    b = 1 + 7 * c

    small = [
        pltpu.make_async_copy(src, dst, insem.at[n])
        for n, (src, dst) in enumerate((
            (tok_hbm, tok_ref), (prob_hbm, prob_ref), (expert_hbm, expert_ref),
            (gate_hbm, gate_ref), (up_hbm, up_ref),
        ))
    ]
    for copy in small:
        copy.start()

    def block_copy(i):
        yi = (y + ring_offset(i)) % SIDE
        cols = pl.ds(pl.multiple_of(yi * COLS, 128), COLS)
        return pltpu.make_async_copy(u_hbm.at[:, cols], ub.at[i], usem.at[i])

    @pl.loop(0, SIDE)
    def _(i):
        block_copy(i).start()

    w_copy = pltpu.make_async_copy(w_hbm, wv, wsem)

    barrier = pltpu.get_barrier_semaphore()

    def greet(xi, wi):
        pl.semaphore_signal(barrier, inc=1, device_id=(xi, wi), device_id_type=MESH)

    @pl.loop(1, SIDE)
    def _(o):
        greet((x + o) % SIDE, wide)
        greet((x + o) % SIDE, chip * 2 + 1 - c)
        greet(x, (((y + o) % SIDE) * SIDE + z) * 2 + c)
        greet(x, (y * SIDE + (z + o) % SIDE) * 2 + c)

    greet(x, chip * 2 + 1 - c)

    for copy in small:
        copy.wait()

    total = jnp.zeros((ROWS, 2 * F), F32)
    token_iota = lax.broadcasted_iota(jnp.int32, (ROWS, F), 0)
    for k in range(NBLK):
        rows = pl.ds(k * BLOCK, BLOCK)
        gate = gate_ref[rows, :].astype(F32)
        up = up_ref[rows, :].astype(F32)
        hidden = gate * jax.nn.sigmoid(gate) * up
        weighted = (hidden * across(prob_ref[pl.ds(k, 1), :])).astype(BF16).astype(F32)
        expert = jnp.full((F, F), expert_ref[k], jnp.int32)
        both = jnp.concatenate(
            [jnp.where(expert == e, weighted, 0.0) for e in range(2)], axis=1
        ).astype(BF16)
        hot = jnp.where(token_iota == tok_ref[pl.ds(k, 1), :], 1.0, 0.0).astype(BF16)
        oh[k] = hot
        total = total + jnp.dot(hot, both, preferred_element_type=F32)
    wp[...] = total.astype(BF16)

    def gradient(i):
        block_copy(i).wait()
        yi = (y + ring_offset(i)) % SIDE
        value = lax.dot_general(
            ub[i], wp[...], (((0,), (0,)), ((), ())), preferred_element_type=F32
        )
        g[pl.ds(yi * SIDE, SIDE)] = value.reshape(SIDE, 2, PIECE, 2 * F)

    @pl.loop(0, 3)
    def _(i):
        gradient(i)

    w_copy.start()
    pl.semaphore_wait(barrier, 4 * (SIDE - 1) + 1)

    def pair_copy(r, j, sem):
        far, near = (other_p + ring_offset(r)) % SIDE, (other_q + ring_offset(j)) % SIDE
        idx = b * far + a * near
        return pltpu.make_async_remote_copy(
            src_ref=g.at[idx, 1 - c],
            dst_ref=r0.at[idx],
            send_sem=pair_send,
            recv_sem=r0_sem.at[sem],
            device_id=(x, chip * 2 + 1 - c),
            device_id_type=MESH,
        )

    other_p, other_q = q, p

    def pair_lead(j):
        pair_copy(0, j, j).start()
        pair_copy(1 + starts_plus(j), j, SIDE + j).start()

    def pair_rest(j):
        pair_copy(2 - starts_plus(j), j, 2 * SIDE).start()

    def pair_group(r):
        @pl.loop(0, SIDE)
        def _(j):
            pair_copy(r, j, 2 * SIDE - 2 + r).start()

    def pair_wait(sem, pieces):
        part = r0.at[pl.ds(0, pieces)]
        pltpu.make_async_copy(part, part, r0_sem.at[sem]).wait()

    def slot(d, k, j):
        return 6 * SIDE + j if k == 4 else (d * 3 + k - 1) * SIDE + j

    def ring_copy(d, s, idx):
        step = 1 if d == 0 else SIDE - 1
        to = (a * ((p + step) % SIDE) + b * q) * 2 + c
        return pltpu.make_async_remote_copy(
            src_ref=r0.at[idx],
            dst_ref=rc1.at[s],
            send_sem=ring_send,
            recv_sem=rc1_sem.at[s],
            device_id=(x, to),
            device_id_type=MESH,
        )

    def first_copy(d, k, j, idx):
        return ring_copy(d, slot(d, k, j), idx)

    def lead_send(j):
        m = starts_plus(j)
        near = b * ((q + ring_offset(j)) % SIDE)
        pair_wait(j, 1)
        pair_wait(SIDE + j, 1)
        for d, far, s in (
            (0, p + 3 + m, m * slot(0, 4, j) + (1 - m) * slot(0, 3, j)),
            (1, p + 4 + m, (1 - m) * slot(1, 4, j) + m * slot(1, 3, j)),
        ):
            idx = a * (far % SIDE) + near
            r0[idx] = r0[idx] + g[idx, c]
            ring_copy(d, s, idx).start()

    def first_send(d, k, j):
        step = 1 if d == 0 else SIDE - 1
        idx = a * ((p + step * k) % SIDE) + b * ((q + ring_offset(j)) % SIDE)
        first_copy(d, k + 1, j, idx).wait_recv()
        r0[idx] = r0[idx] + g[idx, c] + rc1[slot(d, k + 1, j)]
        first_copy(d, k, j, idx).start()

    def project(i):
        yi = (y + ring_offset(i)) % SIDE
        wf[...] = wv[pl.ds(pl.multiple_of(yi * 2 * COLS, 16), 2 * COLS), :].astype(F32)
        weight = jnp.concatenate(
            [wf[pl.ds(e, COLS, stride=2), :].astype(BF16) for e in range(2)], axis=1
        )
        pacc[...] += jnp.dot(ub[i], weight, preferred_element_type=F32)

    pair_lead(0)
    pair_lead(1)

    @pl.loop(3, SIDE)
    def _(i):
        gradient(i)
        pair_lead(i - 1)
        pair_rest(i - 3)

        @pl.when(i >= 4)
        def _():
            lead_send(i - 4)

    pair_lead(7)
    lead_send(4)

    @pl.loop(5, SIDE)
    def _(j):
        pair_rest(j)

    pair_group(3)
    lead_send(5)
    pair_group(4)
    lead_send(6)
    lead_send(7)

    @pl.loop(5, SIDE)
    def _(r):
        pair_group(r)

    w_copy.wait()
    pacc[...] = jnp.zeros_like(pacc)

    def exchange(buf, mine, count, send, recv, order, where):
        @pl.loop(0, count - 1)
        def _(t):
            pltpu.make_async_remote_copy(
                src_ref=buf.at[mine],
                dst_ref=buf.at[mine],
                send_sem=send,
                recv_sem=recv,
                device_id=where(order(t)),
                device_id_type=MESH,
            ).start()

    def exchanged(buf, count, sem):
        part = buf.at[pl.ds(0, count - 1)]
        pltpu.make_async_copy(part, part, sem).wait()

    def rows_back():
        high = pacc[...].astype(BF16)
        rest = pacc[...] - high.astype(F32)
        middle = rest.astype(BF16)
        low = (rest - middle.astype(F32)).astype(BF16)
        pslot[x] = jnp.zeros((8, F), F32)
        for k in range(NBLK):
            rows = pl.ds(k * BLOCK, BLOCK)
            hot = oh[k]
            moved = sum(
                lax.dot_general(hot, term, (((0,), (0,)), ((), ())), preferred_element_type=F32)
                for term in (low, middle, high)
            )
            expert = jnp.full((F, F), expert_ref[k], jnp.int32)
            projected = jnp.where(expert == 0, moved[:, :F], moved[:, F:])
            gate = gate_ref[rows, :].astype(F32)
            up = up_ref[rows, :].astype(F32)
            sig = jax.nn.sigmoid(gate)
            active = gate * sig
            scaled = across(prob_ref[pl.ds(k, 1), :]) * projected
            ugrad_ref[rows, :] = (scaled * active).astype(BF16)
            ggrad_ref[rows, :] = (scaled * up * sig * (1.0 + gate * (1.0 - sig))).astype(BF16)
            part = jnp.transpose(active * up * projected)
            pslot[x, pl.ds(k, 1), :] = jnp.sum(part, axis=0, keepdims=True)

        exchange(pslot, x, SIDE, p_send, p_recv, ring_from(x), lambda to: (to, wide))

    def second_slot(d, k):
        return d * 4 + k - 1

    def second_copy(d, k, idx):
        step = 1 if d == 0 else SIDE - 1
        to = (a * p + b * ((q + step) % SIDE)) * 2 + c
        s = second_slot(d, k)
        return pltpu.make_async_remote_copy(
            src_ref=r0.at[idx],
            dst_ref=rc2.at[s],
            send_sem=ring_send,
            recv_sem=rc2_sem.at[s],
            device_id=(x, to),
            device_id_type=MESH,
        )

    def own(j):
        idx = a * p + b * ((q + ring_offset(j)) % SIDE)
        first_copy(0, 1, j, idx).wait_recv()
        first_copy(1, 1, j, idx).wait_recv()
        return idx, r0[idx] + g[idx, c] + rc1[slot(0, 1, j)] + rc1[slot(1, 1, j)]

    def second_send(j, d, k):
        idx, value = own(j)
        if (d, k) not in ((0, 4), (1, 3)):
            second_copy(d, k + 1, idx).wait_recv()
            value = value + rc2[second_slot(d, k + 1)]
        r0[idx] = value
        second_copy(d, k, idx).start()

    plus = (
        (2, 0), (3, 2), (3, 1), (3, 4), (1, 0), (2, 2), (2, 1), (2, 4), (3, 3), (1, 2),
        (1, 1), (1, 4), (2, 3), (2, 6), (2, 5), (2, 7), (1, 3), (1, 6), (1, 5), (1, 7),
    )
    minus = (
        (3, 0), (2, 2), (2, 1), (2, 4), (2, 0), (1, 2), (1, 1), (1, 4), (1, 0), (2, 3),
        (3, 6), (3, 5), (3, 7), (1, 3), (2, 6), (2, 5), (2, 7), (1, 6), (1, 5), (1, 7),
    )
    for n in range(len(plus)):
        if n == 0:
            for r in (2, 3, 4):
                pair_wait(2 * SIDE - 2 + r, SIDE)
        if n == 4:
            for r in (5, 6):
                pair_wait(2 * SIDE - 2 + r, SIDE)
        first_send(0, *plus[n])
        first_send(1, *minus[n])
        if n in (0, 2, 4, 6):
            @pl.loop(n, n + 2)
            def _(i):
                project(i)
        if n == 8:
            rows_back()
        if n == 14:
            pair_wait(3 * SIDE - 3, SIDE)
            second_send(0, 0, 4)
        if n == 15:
            second_send(2, 1, 3)
        if n == 16:
            second_send(1, 0, 3)
        if n == 18:
            second_send(4, 1, 2)
    second_send(3, 0, 2)
    second_send(6, 1, 1)
    second_send(5, 0, 1)
    idx, value = own(7)
    for d in range(2):
        second_copy(d, 1, idx).wait_recv()
        value = value + rc2[second_slot(d, 1)]
    down_ref[0] = value[:, :F]
    down_ref[1] = value[:, F:]
    column = jnp.sum(value * value, axis=0, keepdims=True)
    square = jnp.concatenate([column[:, :F], column[:, F:]], axis=0)

    stages = (
        (
            qxc, x * 2 + c, 2 * SIDE, xc_send, xc_recv,
            lambda t: ((x + ring_offset(t // 2)) % SIDE) * 2 + (c + 1 + t) % 2,
            lambda to: (to // 2, chip * 2 + to % 2),
        ),
        (
            qy, y, SIDE, y_send, y_recv, ring_from(y),
            lambda to: (x, (to * SIDE + z) * 2 + c),
        ),
        (
            qz, z, SIDE, z_send, z_recv, ring_from(z),
            lambda to: (x, (y * SIDE + to) * 2 + c),
        ),
    )
    for buf, mine, count, send, recv, order, where in stages:
        buf[mine] = square
        exchange(buf, mine, count, send, recv, order, where)
        exchanged(buf, count, recv)
        square = jnp.sum(buf[...], axis=0)
    mean = jnp.sum(square, axis=1, keepdims=True) / float(D * FFW)
    rms_ref[...] = jnp.broadcast_to(jnp.sqrt(mean), (2, F))

    exchanged(pslot, SIDE, p_recv)
    pgrad_ref[...] = jnp.sum(pslot[...], axis=0)

    exchanged(pslot, SIDE, p_send)
    for buf, _, count, send, _, _, _ in stages:
        exchanged(buf, count, send)
    pltpu.make_async_copy(r0, r0, pair_send).wait()
    pltpu.make_async_copy(r0.at[pl.ds(0, 63)], r0.at[pl.ds(0, 63)], ring_send).wait()


def place(down_ref, rms_ref, pgrad_ref, ggrad_ref, ugrad_ref, down, rms, pgrad, ggrad, ugrad):
    for e in range(2):
        down[:, e, :] = down_ref[e]
    lane = lax.broadcasted_iota(jnp.int32, (1, F), 1)
    rms[...] = jnp.where(lane == 0, rms_ref[0:1, :], rms_ref[1:2, :])[:, :2]
    pgrad[...] = pgrad_ref[0:NBLK, :]
    ggrad[...] = ggrad_ref[...]
    ugrad[...] = ugrad_ref[...]


def body(upstream, gate_pre, up_pre, down_weight, block_expert, row_token, gate_prob):
    vmem = pl.BlockSpec(memory_space=pltpu.VMEM)
    hbm = pl.BlockSpec(memory_space=pl.ANY)
    dma = pltpu.SemaphoreType.DMA
    results = pl.pallas_call(
        kernel,
        name="experts_backward",
        out_shape=(
            jax.ShapeDtypeStruct((2, PIECE, F), F32),
            jax.ShapeDtypeStruct((2, F), F32),
            jax.ShapeDtypeStruct((8, F), F32),
            jax.ShapeDtypeStruct((ROWS, F), BF16),
            jax.ShapeDtypeStruct((ROWS, F), BF16),
        ),
        in_specs=[hbm] * 7,
        out_specs=(vmem,) * 5,
        scratch_shapes=[
            pltpu.VMEM((ROWS, F), BF16),
            pltpu.VMEM((ROWS, F), BF16),
            pltpu.VMEM((NBLK, BLOCK), F32),
            pltpu.VMEM((NBLK, BLOCK), jnp.int32),
            pltpu.SMEM((NBLK,), jnp.int32),
            pltpu.VMEM((SIDE, ROWS, COLS), BF16),
            pltpu.VMEM((2 * D, F), BF16),
            pltpu.VMEM((64, 2, PIECE, 2 * F), F32),
            pltpu.VMEM((64, PIECE, 2 * F), F32),
            pltpu.VMEM((56, PIECE, 2 * F), F32),
            pltpu.VMEM((8, PIECE, 2 * F), F32),
            pltpu.VMEM((2 * COLS, F), F32),
            pltpu.VMEM((ROWS, 2 * F), F32),
            pltpu.VMEM((ROWS, 2 * F), BF16),
            pltpu.VMEM((NBLK, ROWS, F), BF16),
            pltpu.VMEM((SIDE, 8, F), F32),
            pltpu.VMEM((2 * SIDE, 2, F), F32),
            pltpu.VMEM((SIDE, 2, F), F32),
            pltpu.VMEM((SIDE, 2, F), F32),
            dma((5,)), dma((SIDE,)), dma, dma, dma((3 * SIDE - 2,)), dma, dma((56,)), dma((8,)),
            dma, dma, dma, dma, dma, dma, dma, dma,
        ],
        compiler_params=pltpu.CompilerParams(
            collective_id=0, has_side_effects=True, vmem_limit_bytes=VMEM_LIMIT * 1024 * 1024
        ),
    )(
        upstream,
        down_weight.reshape(2 * D, F),
        gate_pre,
        up_pre,
        gate_prob.reshape(NBLK, BLOCK),
        row_token.reshape(NBLK, BLOCK),
        block_expert,
    )
    down, rms, pgrad, ggrad, ugrad = pl.pallas_call(
        place,
        name="place_results",
        out_shape=(
            jax.ShapeDtypeStruct((PIECE, 2, F), F32),
            jax.ShapeDtypeStruct((1, 2), F32),
            jax.ShapeDtypeStruct((NBLK, BLOCK), F32),
            jax.ShapeDtypeStruct((ROWS, F), BF16),
            jax.ShapeDtypeStruct((ROWS, F), BF16),
        ),
        in_specs=[vmem] * 5,
        out_specs=(vmem,) * 5,
    )(*results)
    return down, rms.reshape(2), pgrad.reshape(ROWS), ggrad, ugrad


def solution(mesh):
    in_specs = (
        P("wide", None),
        P("wide", "blk"),
        P("wide", "blk"),
        P(None, None, "blk"),
        P("wide"),
        P("wide"),
        P("wide"),
    )
    out_specs = (P("wide", None, "blk"), P(), P("wide"), P("wide", "blk"), P("wide", "blk"))
    return jax.shard_map(body, mesh=mesh, in_specs=in_specs, out_specs=out_specs, check_vma=False)
```
